256 devices in a mesh: row: 16 (over y_lo, x, core), col: 16 (over z, y_hi).
Axes of the slice: x: 4, y: 4 (y_hi: 2, y_lo: 2; y = y_hi * 2 + y_lo), z: 8, core: 2. Of those that a mesh axis runs over, the one named last changes fastest.
Arguments:
- counts: int32 [16, 16, 6, 8, 128, 128], P('row', 'col'), may hold values from 0 to 5
- block_coords: int32 [3, 16, 16, 6], P(None, 'row', 'col'), may hold values from 0 to 127, as said below
- block_count: int32 [16, 16], P('row', 'col'), may hold values from 1 to 6, as said below
- factor_a: float32 [32768, 128], P(('row', 'col')), may hold values from -0.6 to 0.6
- factor_b: float32 [32768, 128], P(('col', 'row')), may hold values from -0.6 to 0.6
- factor_c: float32 [1024, 128], replicated, may hold values from -0.6 to 0.6
Outputs:
- updated_a: float32 [32768, 128], P(('row', 'col'))
- updated_b: float32 [32768, 128], P(('col', 'row'))
The draws below stay inside these ranges and needn't reach their ends.
Inputs may be any that keep to these rules, and one draw needn't show every extreme that they name: `block_coords`: the slots of one cell name distinct blocks; the first index is below 16, the second below 16, the third below 128. `block_count`: at least one cell has all 6 slots live in every draw.
All inputs are finite; a program needn't handle non-finite values.
Results may differ from the reference program's by a relative error of at most 0.0003.
Values sent between devices are 32-bit elements; how exact they have to be, the bound alone decides.
No kernel may reach another device: no remote copies, remote signals or barrier semaphores. Data moves between devices by JAX's collectives and lax.ppermute only.
A program may use at most 64 MiB of HBM per device.

```python
import jax
import jax.numpy as jnp
from jax import lax

R = 128
K = 1024
BS = 128
BK = 8
IBLK = 16
JBLK = 16
SLOTS = 6
STEPS = 2
I = 32768
J = 32768
N_ROW = 16
N_COL = 16


def draw_block_coords(key, part):
    depth_blocks = K // BK
    per_band = IBLK * JBLK * depth_blocks
    cell_keys = jax.random.split(key, N_ROW * N_COL)
    chosen = jax.vmap(lambda cell_key: jax.random.permutation(cell_key, per_band)[:SLOTS])(cell_keys)
    block_i = chosen // (JBLK * depth_blocks)
    block_j = chosen // depth_blocks % JBLK
    block_k = chosen % depth_blocks
    stacked = jnp.stack([block_i, block_j, block_k])
    return stacked.reshape(3, N_ROW, N_COL, SLOTS).astype(jnp.int32)


def draw_block_count(key, part):
    upper_draw = jax.random.randint(jax.random.fold_in(key, 11), (N_ROW * N_COL,), 1, SLOTS + 1)
    lower_draw = jax.random.randint(jax.random.fold_in(key, 12), (N_ROW * N_COL,), 1, SLOTS + 1)
    flattened = jnp.minimum(upper_draw, lower_draw)
    chosen = jax.random.randint(jax.random.fold_in(key, 13), (), 0, N_ROW * N_COL)
    flattened = flattened.at[chosen].set(SLOTS)
    return flattened.reshape(N_ROW, N_COL).astype(jnp.int32)


def with_ends(array, own_key, smallest, largest):
    shape = array.shape
    spot = [jax.random.randint(jax.random.fold_in(own_key, axis), (), 0, shape[axis]) for axis in range(len(shape))]
    array = array.at[tuple(spot)].set(smallest)
    longest = shape.index(max(shape))
    spot[longest] = (spot[longest] + 1) % shape[longest]
    return array.at[tuple(spot)].set(largest)


def block_scale(rng, dims, cuts, smallest, high):
    gain = 1.0
    for position, parts in cuts:
        heights = jax.random.uniform(jax.random.fold_in(jax.random.fold_in(rng, 6), position), (parts,), jnp.float32, smallest / len(cuts), high / len(cuts))
        gain = gain * jnp.repeat(jnp.exp(heights), dims[position] // parts).reshape((-1,) + (1,) * (len(dims) - 1 - position))
    return gain


def setup_inputs(seed: int = 0) -> dict:
    splits = jax.random.split(jax.random.key(seed), 7)
    counts = with_ends(jax.random.randint(splits[0], (N_ROW, N_COL, SLOTS, BK, BS, BS), 0, 6), jax.random.fold_in(splits[0], 1), 0, 5).astype(jnp.int32)
    block_coords = draw_block_coords(jax.random.fold_in(splits[6], 71), 0)
    block_count = draw_block_count(jax.random.fold_in(splits[6], 71), 0)
    factor_a = jnp.clip(jax.random.uniform(splits[3], (I, R), jnp.float32, -0.6, 0.6) * block_scale(splits[3], (I, R), ((0, 256),), -0.4, 0.0), -0.6, 0.6)
    factor_b = jnp.clip(jax.random.uniform(splits[4], (J, R), jnp.float32, -0.6, 0.6) * block_scale(splits[4], (J, R), ((0, 256),), -0.4, 0.0), -0.6, 0.6)
    factor_c = jnp.clip(jax.random.uniform(splits[5], (K, R), jnp.float32, -0.6, 0.6), -0.6, 0.6)
    return {"counts": counts, "block_coords": block_coords, "block_count": block_count, "factor_a": factor_a, "factor_b": factor_b, "factor_c": factor_c}


step_rate = 0.004
highest = lax.Precision.HIGHEST


def block_gradient(piece_a, piece_b, piece_c, observed, valid_flag):
    depth = piece_c.shape[0]
    side = piece_a.shape[0]
    rank = piece_a.shape[1]
    scaled_a = (piece_c[:, None, :] * piece_a[None, :, :]).reshape(depth * side, rank)
    model = jnp.dot(scaled_a, piece_b.T, precision=highest, preferred_element_type=jnp.float32)
    residual = (jnp.exp(model) - observed.reshape(depth * side, side).astype(jnp.float32)) * valid_flag
    scaled_b = piece_c[:, None, :] * piece_b[None, :, :]
    grad_a = jnp.einsum("kab,kbr->ar", residual.reshape(depth, side, side), scaled_b, precision=highest)
    grad_b = jnp.dot(residual.T, scaled_a, precision=highest, preferred_element_type=jnp.float32)
    return grad_a, grad_b


def gradients(factor_a, factor_b, factor_c, counts, block_coords, block_count):
    band_i = IBLK * BS
    band_j = JBLK * BS

    def visit_cell(totals, cell_index):
        total_a, total_b = totals
        row_index = (cell_index // N_COL).astype(jnp.int32)
        col_index = (cell_index % N_COL).astype(jnp.int32)
        band_a = lax.dynamic_slice_in_dim(factor_a, row_index * band_i, band_i, 0)
        band_b = lax.dynamic_slice_in_dim(factor_b, col_index * band_j, band_j, 0)

        def visit_slot(partial_value, slot_index):
            grad_a, grad_b = partial_value
            start_a = (block_coords[0, row_index, col_index, slot_index] * BS).astype(jnp.int32)
            start_b = (block_coords[1, row_index, col_index, slot_index] * BS).astype(jnp.int32)
            start_c = (block_coords[2, row_index, col_index, slot_index] * BK).astype(jnp.int32)
            valid_flag = (slot_index < block_count[row_index, col_index]).astype(jnp.float32)
            piece_a = lax.dynamic_slice_in_dim(band_a, start_a, BS, 0)
            piece_b = lax.dynamic_slice_in_dim(band_b, start_b, BS, 0)
            piece_c = lax.dynamic_slice_in_dim(factor_c, start_c, BK, 0)
            observed = counts[row_index, col_index, slot_index]
            block_a, block_b = block_gradient(piece_a, piece_b, piece_c, observed, valid_flag)
            old_a = lax.dynamic_slice_in_dim(grad_a, start_a, BS, 0)
            old_b = lax.dynamic_slice_in_dim(grad_b, start_b, BS, 0)
            grad_a = lax.dynamic_update_slice_in_dim(grad_a, old_a + block_a, start_a, 0)
            grad_b = lax.dynamic_update_slice_in_dim(grad_b, old_b + block_b, start_b, 0)
            return (grad_a, grad_b), None

        empty_a = jnp.zeros((band_i, R), jnp.float32)
        empty_b = jnp.zeros((band_j, R), jnp.float32)
        (grad_a, grad_b), unused = lax.scan(visit_slot, (empty_a, empty_b), jnp.arange(SLOTS, dtype=jnp.int32))
        old_a = lax.dynamic_slice_in_dim(total_a, row_index * band_i, band_i, 0)
        old_b = lax.dynamic_slice_in_dim(total_b, col_index * band_j, band_j, 0)
        total_a = lax.dynamic_update_slice_in_dim(total_a, old_a + grad_a, row_index * band_i, 0)
        total_b = lax.dynamic_update_slice_in_dim(total_b, old_b + grad_b, col_index * band_j, 0)
        return (total_a, total_b), None

    start = (jnp.zeros_like(factor_a), jnp.zeros_like(factor_b))
    (total_a, total_b), unused = lax.scan(visit_cell, start, jnp.arange(N_ROW * N_COL, dtype=jnp.int32))
    return total_a, total_b


def reference(counts, block_coords, block_count, factor_a, factor_b, factor_c):
    for step_index in range(STEPS):
        grad_a, grad_b = gradients(factor_a, factor_b, factor_c, counts, block_coords, block_count)
        factor_a = factor_a - step_rate * grad_a
        factor_b = factor_b - step_rate * grad_b
    return factor_a, factor_b
```

```python
import functools

import jax
import jax.numpy as jnp
from jax import lax
from jax.experimental import pallas as pl
from jax.experimental.pallas import tpu as pltpu
from jax.sharding import PartitionSpec as P

STEPS = 2
step_rate = 0.004


def split(value):
    high = value.astype(jnp.bfloat16)
    low = (value - high.astype(jnp.float32)).astype(jnp.bfloat16)
    return high, low


def two_halves(value):
    high, low = split(value)
    return jnp.concatenate([high, low], axis=1)


def pair_table(value):
    high, low = split(value)
    row = jnp.concatenate([high, low], axis=1)
    return jnp.concatenate([row, row], axis=0)


def fold(product):
    return product[:, :128] + product[:, 128:]


def gradient_kernel(where_ref, live_ref, a_ref, b_ref, c_ref, counts_ref, ga_ref, gb_ref, seen, sems):
    slots, depth, side, rank = counts_ref.shape
    pieces = a_ref.shape[0]
    live = live_ref[0]

    def fetch(slot):
        return pltpu.make_async_copy(counts_ref.at[slot], seen.at[slot], sems.at[slot])

    for slot in range(slots):

        @pl.when(slot < live)
        def _():
            fetch(slot).start()

    def visit(slot, carry):
        start_c = pl.multiple_of(where_ref[2 * slots + slot] * depth, depth)
        piece_a = a_ref[:, slot].reshape(side, rank)
        piece_b = b_ref[:, slot].reshape(side, rank)
        piece_c = c_ref[pl.ds(start_c, depth), :]
        scaled_a = (piece_c[:, None, :] * piece_a[None, :, :]).reshape(depth * side, rank)
        b_high, b_low = split(piece_b)
        b_rows = jnp.concatenate(
            [jnp.concatenate([b_high, b_high], axis=1), jnp.concatenate([b_low, b_low], axis=1)], axis=0
        )
        model = fold(
            lax.dot_general(
                two_halves(scaled_a), b_rows, (((1,), (1,)), ((), ())), preferred_element_type=jnp.float32
            )
        )
        fetch(slot).wait()
        observed = seen[slot].reshape(depth * side, side)
        residual = jnp.exp(model) - observed.astype(jnp.float32)
        along_b = fold(jnp.dot(two_halves(residual), pair_table(piece_b), preferred_element_type=jnp.float32))
        turned = jnp.swapaxes(residual.reshape(depth, side, side), 1, 2).reshape(depth * side, side)
        along_a = fold(jnp.dot(two_halves(turned), pair_table(piece_a), preferred_element_type=jnp.float32))
        grad_a = (along_b.reshape(depth, side, rank) * piece_c[:, None, :]).sum(0)
        grad_b = (along_a.reshape(depth, side, rank) * piece_c[:, None, :]).sum(0)
        ga_ref[:, slot] = grad_a.reshape(pieces, side // pieces, rank)
        gb_ref[:, slot] = grad_b.reshape(pieces, side // pieces, rank)
        return carry

    lax.fori_loop(0, live, visit, 0)

    def clear(slot, carry):
        ga_ref[:, slot] = jnp.zeros((pieces, side // pieces, rank), jnp.float32)
        gb_ref[:, slot] = jnp.zeros((pieces, side // pieces, rank), jnp.float32)
        return carry

    lax.fori_loop(live, slots, clear, 0)


def block_gradients(where, live, a, b, c, counts):
    slots = counts.shape[0]
    vmem = pl.BlockSpec(memory_space=pltpu.VMEM)
    smem = pl.BlockSpec(memory_space=pltpu.SMEM)
    return pl.pallas_call(
        gradient_kernel,
        out_shape=(jax.ShapeDtypeStruct(a.shape, jnp.float32), jax.ShapeDtypeStruct(b.shape, jnp.float32)),
        in_specs=[smem, smem, vmem, vmem, vmem, pl.BlockSpec(memory_space=pl.ANY)],
        out_specs=(vmem, vmem),
        scratch_shapes=[pltpu.VMEM(counts.shape, jnp.int32), pltpu.SemaphoreType.DMA((slots,))],
        cost_estimate=pl.CostEstimate(flops=1 << 30, bytes_accessed=6 << 20, transcendentals=1 << 20),
    )(where, live, a, b, c, counts)


def deal_kernel(wanted_ref, piece_ref, out_ref):
    members, slots = out_ref.shape[:2]
    for member in range(members):
        for slot in range(slots):
            block = jnp.minimum(wanted_ref[member * slots + slot], members - 1)
            out_ref[member, slot] = piece_ref[block]


def deal(wanted, pieces, slots):
    members, rows, rank = pieces.shape
    vmem = pl.BlockSpec(memory_space=pltpu.VMEM)
    return pl.pallas_call(
        deal_kernel,
        out_shape=jax.ShapeDtypeStruct((members, slots, rows, rank), jnp.float32),
        in_specs=[pl.BlockSpec(memory_space=pltpu.SMEM), vmem],
        out_specs=vmem,
        cost_estimate=pl.CostEstimate(flops=1 << 20, bytes_accessed=1 << 20, transcendentals=0),
    )(wanted, pieces)


def update_kernel(again, wanted_ref, piece_ref, grad_ref, *rest):
    new_ref, total = rest[0], rest[-1]
    members, slots = grad_ref.shape[:2]
    total[...] = jnp.zeros_like(total)
    for member in range(members):
        for slot in range(slots):
            block = wanted_ref[member * slots + slot]
            total[block] = total[block] + grad_ref[member, slot]
    new_ref[...] = piece_ref[...] - step_rate * total[:members]
    if again:
        deal_kernel(wanted_ref, new_ref, rest[1])


def update(wanted, pieces, grads, again):
    members, rows, rank = pieces.shape
    vmem = pl.BlockSpec(memory_space=pltpu.VMEM)
    shapes = [jax.ShapeDtypeStruct(pieces.shape, jnp.float32)]
    if again:
        shapes.append(jax.ShapeDtypeStruct(grads.shape, jnp.float32))
    return pl.pallas_call(
        functools.partial(update_kernel, again),
        out_shape=shapes,
        in_specs=[pl.BlockSpec(memory_space=pltpu.SMEM), vmem, vmem],
        out_specs=[vmem] * len(shapes),
        scratch_shapes=[pltpu.VMEM((members + 1, rows, rank), jnp.float32)],
        cost_estimate=pl.CostEstimate(flops=1 << 20, bytes_accessed=1 << 20, transcendentals=0),
    )(wanted, pieces, grads)


def swap(value, axis):
    return lax.all_to_all(value, axis, 0, 0, tiled=True)


def spread(factor, named, axis, members):
    slots = named.shape[0]
    rows, rank = factor.shape
    note = jnp.zeros((rank,), jnp.float32).at[:slots].set(named.astype(jnp.float32))
    pieces = factor.reshape(members, rows // members, rank)
    sent = jnp.concatenate([pieces, jnp.broadcast_to(note, pieces.shape)], axis=1)
    got = swap(sent, axis)
    wanted = got[:, rows // members, :slots].astype(jnp.int32).reshape(members * slots)
    return got[:, : rows // members], wanted


def local(counts, block_coords, block_count, factor_a, factor_b, factor_c):
    slots = counts.shape[2]
    members_a, members_b = lax.axis_size("col"), lax.axis_size("row")
    where = block_coords.reshape(3 * slots)
    live = block_count.reshape(1)
    counts = counts.reshape(counts.shape[2:])
    alive = jnp.arange(slots, dtype=jnp.int32) < live
    pieces_b, wanted_b = spread(factor_b, jnp.where(alive, where[slots : 2 * slots], members_b), "row", members_b)
    pieces_a, wanted_a = spread(factor_a, jnp.where(alive, where[:slots], members_a), "col", members_a)
    dealt_b = deal(wanted_b, pieces_b, slots)
    dealt_a = deal(wanted_a, pieces_a, slots)
    for step_index in range(STEPS):
        held_b = swap(dealt_b, "row")
        held_a = swap(dealt_a, "col")
        grad_a, grad_b = block_gradients(where, live, held_a, held_b, factor_c, counts)
        back_b = swap(grad_b, "row")
        back_a = swap(grad_a, "col")
        again = step_index + 1 < STEPS
        pieces_b, *dealt_b = update(wanted_b, pieces_b, back_b, again)
        pieces_a, *dealt_a = update(wanted_a, pieces_a, back_a, again)
        if again:
            dealt_a, dealt_b = dealt_a[0], dealt_b[0]
    new_b = swap(pieces_b, "row").reshape(factor_b.shape)
    new_a = swap(pieces_a, "col").reshape(factor_a.shape)
    return (new_a, new_b)


def solution(mesh):
    return jax.shard_map(
        local,
        mesh=mesh,
        in_specs=(
            P("row", "col", None, None, None, None),
            P(None, "row", "col", None),
            P("row", "col"),
            P(("row", "col"), None),
            P(("col", "row"), None),
            P(),
        ),
        out_specs=(P(("row", "col"), None), P(("col", "row"), None)),
        check_vma=False,
    )
```

```python
import functools

import jax
import jax.numpy as jnp
from jax import lax
from jax.experimental import pallas as pl
from jax.experimental.pallas import tpu as pltpu
from jax.sharding import PartitionSpec as P


STEPS = 2
step_rate = 0.004


vmem = pl.BlockSpec(memory_space=pltpu.VMEM)
smem = pl.BlockSpec(memory_space=pltpu.SMEM)
anywhere = pl.BlockSpec(memory_space=pl.ANY)
small_cost = pl.CostEstimate(flops=1 << 20, bytes_accessed=1 << 20, transcendentals=0)
chip_order = (6, 7, 5, 2, 4, 3, 1)


def shape_of(*sizes):
    return jax.ShapeDtypeStruct(sizes, jnp.float32)


def rows_at(index, rows):
    return pl.ds(pl.multiple_of(index * rows, rows), rows)


def split(value):
    high = value.astype(jnp.bfloat16)
    low = (value - high.astype(jnp.float32)).astype(jnp.bfloat16)
    return high, low


def two_halves(value):
    high, low = split(value)
    return jnp.concatenate([high, low], axis=1)


def pair_table(value):
    row = two_halves(value)
    return jnp.concatenate([row, row], axis=0)


def fold(product):
    return product[:, :128] + product[:, 128:]


def swap_col(sent):
    return lax.all_to_all(sent, "col", 0, 0, tiled=True)


def shift_row(value, change):
    members = lax.axis_size("row")
    return lax.ppermute(value, "row", [(member, member ^ change) for member in range(members)])


def swap_row(even, odd):
    passed = shift_row(odd, 1)
    both = [jnp.stack([even[pair], passed[pair]]) for pair in range(even.shape[0])]
    got = [both[0]] + [None] * len(chip_order)
    for pair in chip_order:
        got[pair] = shift_row(both[pair], 2 * pair)
    return got


def open_kernel(where_ref, live_ref, a_ref, b_ref, send_a, send_b):
    slots = where_ref.shape[0] // 3
    side, rank = a_ref.shape
    members = send_a.shape[0]
    rows = send_b.shape[0] - side
    lane = lax.broadcasted_iota(jnp.int32, (rows, rank), 1)

    def note(first):
        value = jnp.zeros((rows, rank), jnp.float32)
        for slot in range(slots):
            named = jnp.where(slot < live_ref[0], where_ref[first + slot], members).astype(jnp.float32)
            value = jnp.where(lane == slot, named, value)
        return value

    send_b[:side] = b_ref[...]
    send_b[side:] = note(slots)
    block, named = a_ref[...], note(0)
    for member in range(members):
        send_a[member, :side] = block
        send_a[member, side:] = named


def open_blocks(where, live, factor_a, factor_b, members):
    side, rank = factor_a.shape
    rows = side // members
    return pl.pallas_call(
        open_kernel,
        out_shape=(shape_of(members, side + rows, rank), shape_of(side + rows, rank)),
        in_specs=[smem, smem, vmem, vmem],
        out_specs=(vmem, vmem),
        cost_estimate=small_cost,
    )(where, live, factor_a, factor_b)


def start_kernel(slots, at_ref, *refs):
    a_ref, b_refs, refs = refs[0], refs[1:9], refs[9:]
    wanted_a, wanted_b, piece_a, piece_b, notes, held, sems = refs
    members, rows, _ = piece_a.shape
    side = members * rows
    copies = [
        pltpu.make_async_copy(a_ref.at[:, rows_at(at_ref[1], rows)], piece_a, sems.at[0]),
        pltpu.make_async_copy(a_ref.at[:, side], notes.at[0], sems.at[1]),
    ]
    for pair, ref in enumerate(b_refs):
        two = pl.ds(2 * pair, 2)
        copies.append(
            pltpu.make_async_copy(ref.at[:, rows_at(at_ref[0], rows)], held.at[two], sems.at[2 + 2 * pair])
        )
        copies.append(pltpu.make_async_copy(ref.at[:, side], notes.at[1, two], sems.at[3 + 2 * pair]))
    for copy in copies:
        copy.start()
    for copy in copies:
        copy.wait()
    for place in range(members):
        piece_b[at_ref[0] ^ place] = held[place]

    def name(place, carry):
        for slot in range(slots):
            wanted_a[place * slots + slot] = notes[0, place, slot].astype(jnp.int32)
            wanted_b[place * slots + slot] = notes[1, place, slot].astype(jnp.int32)
        return carry

    lax.fori_loop(0, members, name, 0)


def start_pieces(at, all_a, all_b, members, slots, rows, rank):
    names = jax.ShapeDtypeStruct((members * slots,), jnp.int32)
    return pl.pallas_call(
        functools.partial(start_kernel, slots),
        out_shape=(names, names, shape_of(members, rows, rank), shape_of(members, rows, rank)),
        in_specs=[smem] + [anywhere] * 9,
        out_specs=(smem, smem, vmem, vmem),
        scratch_shapes=[
            pltpu.SMEM((2, members, rank), jnp.float32),
            pltpu.VMEM((members, rows, rank), jnp.float32),
            pltpu.SemaphoreType.DMA((18,)),
        ],
        cost_estimate=small_cost,
    )(at, all_a, *all_b)


def slot_gradients(piece_a, piece_b, piece_c, observed):
    depth, (side, rank) = piece_c.shape[0], piece_a.shape
    scaled_a = (piece_c[:, None, :] * piece_a[None, :, :]).reshape(depth * side, rank)
    b_high, b_low = split(piece_b)
    b_rows = jnp.concatenate(
        [jnp.concatenate([b_high, b_high], axis=1), jnp.concatenate([b_low, b_low], axis=1)], axis=0
    )
    model = fold(
        lax.dot_general(two_halves(scaled_a), b_rows, (((1,), (1,)), ((), ())), preferred_element_type=jnp.float32)
    )
    residual = jnp.exp(model) - observed().reshape(depth * side, side).astype(jnp.float32)
    along_b = fold(jnp.dot(two_halves(residual), pair_table(piece_b), preferred_element_type=jnp.float32))
    turned = jnp.swapaxes(residual.reshape(depth, side, side), 1, 2).reshape(depth * side, side)
    along_a = fold(jnp.dot(two_halves(turned), pair_table(piece_a), preferred_element_type=jnp.float32))
    grad_a = (along_b.reshape(depth, side, rank) * piece_c[:, None, :]).sum(0)
    grad_b = (along_a.reshape(depth, side, rank) * piece_c[:, None, :]).sum(0)
    return grad_a, grad_b


class Fetches:
    def __init__(self, where_ref, live_ref, c_ref, counts_ref, part_c, seen, sems):
        self.refs = where_ref, live_ref, c_ref, counts_ref, part_c, seen, sems
        self.slots, self.depth = counts_ref.shape[:2]

    def copies(self, slot):
        where_ref, _, c_ref, counts_ref, part_c, seen, sems = self.refs
        start_c = pl.multiple_of(where_ref[2 * self.slots + slot] * self.depth, self.depth)
        return (
            pltpu.make_async_copy(c_ref.at[pl.ds(start_c, self.depth)], part_c.at[slot], sems.at[0, slot]),
            pltpu.make_async_copy(counts_ref.at[slot], seen.at[slot], sems.at[1, slot]),
        )

    def start(self):
        for slot in range(self.slots):

            @pl.when(slot < self.refs[1][0])
            def _():
                for copy in self.copies(slot):
                    copy.start()

    def factor(self, slot):
        self.copies(slot)[0].wait()
        return self.refs[4][slot]

    def observed(self, slot):
        self.copies(slot)[1].wait()
        return self.refs[5][slot]


def first_kernel(at_ref, where_ref, live_ref, *refs):
    a_ref, b_refs, (c_ref, counts_ref), refs = refs[0], refs[1:9], refs[9:11], refs[11:]
    ga_ref, gb_refs, refs = refs[0], refs[1:3], refs[3:]
    block_a, all_b, turned_b, part_c, seen, sems, sem_a, sem_b = refs
    slots, _, side, rank = counts_ref.shape
    members = a_ref.shape[0]
    rows = side // members
    live = live_ref[0]
    fetches = Fetches(where_ref, live_ref, c_ref, counts_ref, part_c, seen, sems)

    def fetch_a(slot):
        return pltpu.make_async_copy(a_ref.at[where_ref[slot], pl.ds(0, side)], block_a.at[slot], sem_a.at[slot])

    copies_b = [
        pltpu.make_async_copy(ref.at[:, pl.ds(0, side)], all_b.at[pl.ds(2 * pair, 2)], sem_b.at[pair])
        for pair, ref in enumerate(b_refs)
    ]
    for slot in range(slots):

        @pl.when(slot < live)
        def _():
            fetch_a(slot).start()

    for copy in copies_b:
        copy.start()
    fetches.start()
    for copy in copies_b:
        copy.wait()

    def visit(slot, carry):
        fetch_a(slot).wait()
        piece_b = all_b[where_ref[slots + slot] ^ at_ref[0]]
        grad_a, grad_b = slot_gradients(
            block_a[slot], piece_b, fetches.factor(slot), functools.partial(fetches.observed, slot)
        )
        ga_ref[:, slot] = grad_a.reshape(members, rows, rank)
        turned_b[...] = grad_b
        for place in range(members):
            gb_refs[place % 2][place // 2, slot] = turned_b[rows_at(at_ref[0] ^ place, rows), :]
        return carry

    lax.fori_loop(0, live, visit, 0)

    def clear(slot, carry):
        ga_ref[:, slot] = jnp.zeros((members, rows, rank), jnp.float32)
        for ref in gb_refs:
            ref[:, slot] = jnp.zeros((members // 2, rows, rank), jnp.float32)
        return carry

    lax.fori_loop(live, slots, clear, 0)


def last_kernel(at_ref, where_ref, live_ref, *refs):
    a_ref, b_refs, (c_ref, counts_ref), refs = refs[0], refs[1:9], refs[9:11], refs[11:]
    ga_ref, even_ref, odd_ref, base_b, refs = *refs[:4], refs[4:]
    block_a, all_b, block_b, part_c, seen, sems, sem_b = refs
    slots, _, side, rank = counts_ref.shape
    members = a_ref.shape[0]
    rows = side // members
    live = live_ref[0]
    me = at_ref[0]
    fetches = Fetches(where_ref, live_ref, c_ref, counts_ref, part_c, seen, sems)
    copies = [pltpu.make_async_copy(a_ref, block_a, sem_b.at[8])]
    for pair, ref in enumerate(b_refs):
        copies.append(pltpu.make_async_copy(ref, all_b.at[pl.ds(2 * pair, 2)], sem_b.at[pair]))
    for copy in copies:
        copy.start()
    fetches.start()
    for ref in (ga_ref, even_ref, odd_ref):
        ref[...] = jnp.zeros_like(ref)
    for copy in copies:
        copy.wait()
    for place in range(members):
        base_b[rows_at(me ^ place, rows), :] = all_b[place, slots]

    def visit(slot, carry):
        for place in range(members):
            block_b[rows_at(me ^ place, rows), :] = all_b[place, slot]
        grad_a, grad_b = slot_gradients(
            block_a[:, slot].reshape(side, rank),
            block_b[...],
            fetches.factor(slot),
            functools.partial(fetches.observed, slot),
        )
        ga_ref[where_ref[slot]] += grad_a
        place = where_ref[slots + slot] ^ me

        @pl.when(place % 2 == 0)
        def _():
            even_ref[place // 2] += grad_b

        @pl.when(place % 2 == 1)
        def _():
            odd_ref[place // 2] += grad_b

        return carry

    lax.fori_loop(0, live, visit, 0)


def block_gradients(at, where, live, held_a, held_b, c, counts, members, last):
    slots, depth, side, rank = counts.shape
    rows = side // members
    common = [
        pltpu.VMEM((slots, depth, rank), jnp.float32),
        pltpu.VMEM(counts.shape, jnp.int32),
        pltpu.SemaphoreType.DMA((2, slots)),
    ]
    if last:
        kernel = last_kernel
        half = shape_of(members // 2, side, rank)
        shapes = (shape_of(members, side, rank), half, half, shape_of(side, rank))
        scratch = [
            pltpu.VMEM(held_a.shape, jnp.float32),
            pltpu.VMEM((members, *held_b[0].shape[1:]), jnp.float32),
            pltpu.VMEM((side, rank), jnp.float32),
            *common,
            pltpu.SemaphoreType.DMA((9,)),
        ]
    else:
        kernel = first_kernel
        half = shape_of(members // 2, slots, rows, rank)
        shapes = (shape_of(members, slots, rows, rank), half, half)
        scratch = [
            pltpu.VMEM((slots, side, rank), jnp.float32),
            pltpu.VMEM((members, side, rank), jnp.float32),
            pltpu.VMEM((side, rank), jnp.float32),
            *common,
            pltpu.SemaphoreType.DMA((slots,)),
            pltpu.SemaphoreType.DMA((8,)),
        ]
    return pl.pallas_call(
        kernel,
        out_shape=shapes,
        in_specs=[smem] * 3 + [anywhere] * 11,
        out_specs=[vmem] * len(shapes),
        scratch_shapes=scratch,
        cost_estimate=pl.CostEstimate(flops=1 << 30, bytes_accessed=6 << 20, transcendentals=1 << 20),
    )(at, where, live, held_a, *held_b, c, counts)


def update_kernel(received, at_ref, wanted_ref, piece_ref, *refs):
    sources, refs = refs[:received], refs[received:]
    outs, (grads, total, sems) = refs[:-3], refs[-3:]
    members, slots, _, _ = grads.shape
    each = members // received
    copies = [
        pltpu.make_async_copy(ref, grads.at[pl.ds(each * index, each)], sems.at[index])
        for index, ref in enumerate(sources)
    ]
    for copy in copies:
        copy.start()
    total[...] = jnp.zeros_like(total)
    for copy in copies:
        copy.wait()

    def gather(place, carry):
        for slot in range(slots):
            block = wanted_ref[place * slots + slot]
            total[block] = total[block] + grads[place, slot]
        return carry

    lax.fori_loop(0, members, gather, 0)
    total[:members] = piece_ref[...] - step_rate * total[:members]

    def deal(index, carry):
        for way, out_ref in enumerate(outs):
            place = index * len(outs) + way
            owner = place if received == 1 else at_ref[0] ^ place
            for slot in range(slots):
                out_ref[index, slot] = total[jnp.minimum(wanted_ref[place * slots + slot], members - 1)]
            out_ref[index, slots] = total[owner]
        return carry

    lax.fori_loop(0, members // len(outs), deal, 0)


def update(at, wanted, pieces, grads):
    members, rows, rank = pieces.shape
    slots = grads[0].shape[1]
    if len(grads) == 1:
        shapes = [shape_of(members, slots + 1, rows, rank)]
    else:
        shapes = [shape_of(members // 2, slots + 1, rows, rank)] * 2
    return pl.pallas_call(
        functools.partial(update_kernel, len(grads)),
        out_shape=shapes,
        in_specs=[smem, smem, vmem] + [anywhere] * len(grads),
        out_specs=[vmem] * len(shapes),
        scratch_shapes=[
            pltpu.VMEM((members, slots, rows, rank), jnp.float32),
            pltpu.VMEM((members + 1, rows, rank), jnp.float32),
            pltpu.SemaphoreType.DMA((len(grads),)),
        ],
        cost_estimate=small_cost,
    )(at, wanted, pieces, *grads)


def local(counts, block_coords, block_count, factor_a, factor_b, factor_c):
    assert STEPS == 2
    slots = counts.shape[2]
    members = lax.axis_size("row")
    side, rank = factor_a.shape
    rows = side // members
    at = jnp.stack([lax.axis_index("row"), lax.axis_index("col")]).astype(jnp.int32)
    where = block_coords.reshape(3 * slots)
    live = block_count.reshape(1)
    counts = counts.reshape(counts.shape[2:])
    send_a, send_b = open_blocks(where, live, factor_a, factor_b, members)
    all_a = swap_col(send_a)
    both = jnp.stack([send_b, shift_row(send_b, 1)])
    all_b = [both] + [None] * len(chip_order)
    for pair in chip_order:
        all_b[pair] = shift_row(both, 2 * pair)
    grad_a, *grad_b = block_gradients(
        at, where, live, all_a, all_b, factor_c, counts, members, False
    )
    wanted_a, wanted_b, pieces_a, pieces_b = start_pieces(at, all_a, all_b, members, slots, rows, rank)
    back_a = swap_col(grad_a)
    back_b = swap_row(*grad_b)
    dealt_b = update(at, wanted_b, pieces_b, back_b)
    (dealt_a,) = update(at, wanted_a, pieces_a, [back_a])
    held_a = swap_col(dealt_a)
    held_b = swap_row(*dealt_b)
    grad_a, even_b, odd_b, base_b = block_gradients(at, where, live, held_a, held_b, factor_c, counts, members, True)
    terms_a = swap_col(grad_a)
    sums = even_b + shift_row(odd_b, 1)
    terms_b = [sums[0]] + [shift_row(sums[pair], 2 * pair) for pair in chip_order]
    new_b = base_b - step_rate * sum(terms_b)
    new_a = held_a[:, slots].reshape(side, rank) - step_rate * terms_a.sum(0)
    return (new_a, new_b)


def solution(mesh):
    return jax.shard_map(
        local,
        mesh=mesh,
        in_specs=(
            P("row", "col", None, None, None, None),
            P(None, "row", "col", None),
            P("row", "col"),
            P(("row", "col"), None),
            P(("col", "row"), None),
            P(),
        ),
        out_specs=(P(("row", "col"), None), P(("col", "row"), None)),
        check_vma=False,
    )
```

```python
import functools

import jax
import jax.numpy as jnp
from jax import lax
from jax.experimental import pallas as pl
from jax.experimental.pallas import tpu as pltpu
from jax.sharding import PartitionSpec as P


STEPS = 2
step_rate = 0.004


vmem = pl.BlockSpec(memory_space=pltpu.VMEM)
smem = pl.BlockSpec(memory_space=pltpu.SMEM)
anywhere = pl.BlockSpec(memory_space=pl.ANY)
small_cost = pl.CostEstimate(flops=1 << 20, bytes_accessed=1 << 20, transcendentals=0)
parts = 2
chip_order = (6, 7, 5, 2, 4, 3, 1)


def shape_of(*sizes):
    return jax.ShapeDtypeStruct(sizes, jnp.float32)


def rows_at(index, rows):
    return pl.ds(pl.multiple_of(index * rows, rows), rows)


def split(value):
    high = value.astype(jnp.bfloat16)
    low = (value - high.astype(jnp.float32)).astype(jnp.bfloat16)
    return high, low


def two_halves(value):
    high, low = split(value)
    return jnp.concatenate([high, low], axis=1)


def pair_table(value):
    row = two_halves(value)
    return jnp.concatenate([row, row], axis=0)


def fold(product):
    return product[:, :128] + product[:, 128:]


def near(value):
    return pltpu.with_memory_space_constraint(value, pltpu.VMEM)


def swap_col(sent):
    return lax.all_to_all(sent, "col", 0, 0, tiled=True)


def shift_row(value, change):
    members = lax.axis_size("row")
    return lax.ppermute(value, "row", [(member, member ^ change) for member in range(members)])


def swap_row(even, odd):
    passed = shift_row(odd, 1)
    both = [jnp.stack([even[pair], passed[pair]]) for pair in range(even.shape[0])]
    got = [both[0]] + [None] * len(chip_order)
    for pair in chip_order:
        got[pair] = shift_row(both[pair], 2 * pair)
    return got


def open_kernel(where_ref, live_ref, a_ref, b_ref, send_a, send_b):
    slots = where_ref.shape[3]
    side, rank = a_ref.shape
    members = send_a.shape[0]
    rows = send_b.shape[0] - side
    lane = lax.broadcasted_iota(jnp.int32, (rows, rank), 1)

    def note(kind):
        value = jnp.zeros((rows, rank), jnp.float32)
        for slot in range(slots):
            named = jnp.where(slot < live_ref[0, 0], where_ref[kind, 0, 0, slot], members).astype(jnp.float32)
            value = jnp.where(lane == slot, named, value)
        return value

    send_b[:side] = b_ref[...]
    send_b[side:] = note(1)
    block, named = a_ref[...], note(0)
    for member in range(members):
        send_a[member, :side] = block
        send_a[member, side:] = named


def open_blocks(where, live, factor_a, factor_b, members):
    side, rank = factor_a.shape
    rows = side // members
    return pl.pallas_call(
        open_kernel,
        out_shape=(shape_of(members, side + rows, rank), shape_of(side + rows, rank)),
        in_specs=[smem, smem, vmem, vmem],
        out_specs=(vmem, vmem),
        cost_estimate=small_cost,
    )(where, live, factor_a, factor_b)


def slot_gradients(piece_a, piece_b, piece_c, observed):
    depth, (side, rank) = piece_c.shape[0], piece_a.shape
    b_high, b_low = split(piece_b)
    b_rows = jnp.concatenate(
        [jnp.concatenate([b_high, b_high], axis=1), jnp.concatenate([b_low, b_low], axis=1)], axis=0
    )
    b_table, a_table = pair_table(piece_b), pair_table(piece_a)
    counted = observed()
    grad_a = grad_b = jnp.zeros((side, rank), jnp.float32)
    each = depth // parts
    for part in range(parts):
        own = slice(part * each, (part + 1) * each)
        part_c = piece_c[own][:, None, :]
        scaled_a = (part_c * piece_a[None, :, :]).reshape(each * side, rank)
        model = fold(
            lax.dot_general(
                two_halves(scaled_a), b_rows, (((1,), (1,)), ((), ())), preferred_element_type=jnp.float32
            )
        )
        residual = jnp.exp(model) - counted[own].reshape(each * side, side).astype(jnp.float32)
        along_b = fold(jnp.dot(two_halves(residual), b_table, preferred_element_type=jnp.float32))
        turned = jnp.swapaxes(residual.reshape(each, side, side), 1, 2).reshape(each * side, side)
        along_a = fold(jnp.dot(two_halves(turned), a_table, preferred_element_type=jnp.float32))
        grad_a += (along_b.reshape(each, side, rank) * part_c).sum(0)
        grad_b += (along_a.reshape(each, side, rank) * part_c).sum(0)
    return grad_a, grad_b


class Fetches:
    def __init__(self, where_ref, live_ref, c_ref, counts_ref, part_c, seen, sems):
        self.refs = where_ref, live_ref, c_ref, counts_ref, part_c, seen, sems
        self.slots, self.depth = counts_ref.shape[:2]

    def copy_c(self, slot):
        where_ref, _, c_ref, _, part_c, _, sems = self.refs
        start_c = pl.multiple_of(where_ref[2, 0, 0, slot] * self.depth, self.depth)
        return pltpu.make_async_copy(c_ref.at[pl.ds(start_c, self.depth)], part_c.at[slot], sems.at[0, slot])

    def copy_counts(self, slot):
        _, _, _, counts_ref, _, seen, sems = self.refs
        return pltpu.make_async_copy(counts_ref.at[slot], seen.at[slot], sems.at[1, slot])

    def start(self):
        for slot in range(self.slots):

            @pl.when(slot < self.refs[1][0, 0])
            def _():
                self.copy_c(slot).start()
                self.copy_counts(slot).start()

    def factor(self, slot):
        self.copy_c(slot).wait()
        return self.refs[4][slot]

    def observed(self, slot):
        self.copy_counts(slot).wait()
        return self.refs[5][slot]


def first_kernel(at_ref, where_ref, live_ref, *refs):
    a_ref, b_refs, (c_ref, counts_ref), refs = refs[0], refs[1:9], refs[9:11], refs[11:]
    ga_ref, gb_refs, refs = refs[0], refs[1:3], refs[3:]
    block_a, all_b, turned_b, part_c, seen, sems, sem_a, sem_b = refs
    slots, _, side, rank = counts_ref.shape
    members = a_ref.shape[0]
    rows = side // members
    live = live_ref[0, 0]
    fetches = Fetches(where_ref, live_ref, c_ref, counts_ref, part_c, seen, sems)

    def fetch_a(slot):
        return pltpu.make_async_copy(a_ref.at[where_ref[0, 0, 0, slot], pl.ds(0, side)], block_a.at[slot], sem_a.at[slot])

    copies_b = [
        pltpu.make_async_copy(ref.at[:, pl.ds(0, side)], all_b.at[pl.ds(2 * pair, 2)], sem_b.at[pair])
        for pair, ref in enumerate(b_refs)
    ]
    for slot in range(slots):

        @pl.when(slot < live)
        def _():
            fetch_a(slot).start()

    for copy in copies_b:
        copy.start()
    fetches.start()
    for copy in copies_b:
        copy.wait()

    def visit(slot, carry):
        fetch_a(slot).wait()
        piece_b = all_b[where_ref[1, 0, 0, slot] ^ at_ref[0]]
        grad_a, grad_b = slot_gradients(
            block_a[slot], piece_b, fetches.factor(slot), functools.partial(fetches.observed, slot)
        )
        ga_ref[:, slot] = grad_a.reshape(members, rows, rank)
        turned_b[...] = grad_b
        for place in range(members):
            gb_refs[place % 2][place // 2, slot] = turned_b[rows_at(at_ref[0] ^ place, rows), :]
        return carry

    lax.fori_loop(0, live, visit, 0)

    def clear(slot, carry):
        ga_ref[:, slot] = jnp.zeros((members, rows, rank), jnp.float32)
        for ref in gb_refs:
            ref[:, slot] = jnp.zeros((members // 2, rows, rank), jnp.float32)
        return carry

    lax.fori_loop(live, slots, clear, 0)


def last_kernel(at_ref, where_ref, live_ref, *refs):
    a_ref, b_refs, (c_ref, counts_ref), refs = refs[0], refs[1:9], refs[9:11], refs[11:]
    ga_ref, even_ref, odd_ref, base_b, refs = *refs[:4], refs[4:]
    block_a, all_b, block_b, part_c, seen, sems, sem_b = refs
    slots, _, side, rank = counts_ref.shape
    members = a_ref.shape[0]
    rows = side // members
    live = live_ref[0, 0]
    me = at_ref[0]
    fetches = Fetches(where_ref, live_ref, c_ref, counts_ref, part_c, seen, sems)
    copies = [pltpu.make_async_copy(a_ref, block_a, sem_b.at[8])]
    for pair, ref in enumerate(b_refs):
        copies.append(pltpu.make_async_copy(ref, all_b.at[pl.ds(2 * pair, 2)], sem_b.at[pair]))
    for copy in copies:
        copy.start()
    fetches.start()
    for ref in (ga_ref, even_ref, odd_ref):
        ref[...] = jnp.zeros_like(ref)
    for copy in copies:
        copy.wait()
    for place in range(members):
        base_b[rows_at(me ^ place, rows), :] = all_b[place, slots]

    def visit(slot, carry):
        for place in range(members):
            block_b[rows_at(me ^ place, rows), :] = all_b[place, slot]
        grad_a, grad_b = slot_gradients(
            block_a[:, slot].reshape(side, rank),
            block_b[...],
            fetches.factor(slot),
            functools.partial(fetches.observed, slot),
        )
        ga_ref[where_ref[0, 0, 0, slot]] += grad_a
        place = where_ref[1, 0, 0, slot] ^ me

        @pl.when(place % 2 == 0)
        def _():
            even_ref[place // 2] += grad_b

        @pl.when(place % 2 == 1)
        def _():
            odd_ref[place // 2] += grad_b

        return carry

    lax.fori_loop(0, live, visit, 0)


def block_gradients(at, where, live, held_a, held_b, c, counts, members, last):
    slots, depth, side, rank = counts.shape
    rows = side // members
    common = [
        pltpu.VMEM((slots, depth, rank), jnp.float32),
        pltpu.VMEM(counts.shape, jnp.int32),
        pltpu.SemaphoreType.DMA((2, slots)),
    ]
    if last:
        kernel = last_kernel
        half = shape_of(members // 2, side, rank)
        shapes = (shape_of(members, side, rank), half, half, shape_of(side, rank))
        scratch = [
            pltpu.VMEM(held_a.shape, jnp.float32),
            pltpu.VMEM((members, *held_b[0].shape[1:]), jnp.float32),
            pltpu.VMEM((side, rank), jnp.float32),
            *common,
            pltpu.SemaphoreType.DMA((9,)),
        ]
    else:
        kernel = first_kernel
        half = shape_of(members // 2, slots, rows, rank)
        shapes = (shape_of(members, slots, rows, rank), half, half)
        scratch = [
            pltpu.VMEM((slots, side, rank), jnp.float32),
            pltpu.VMEM((members, side, rank), jnp.float32),
            pltpu.VMEM((side, rank), jnp.float32),
            *common,
            pltpu.SemaphoreType.DMA((slots,)),
            pltpu.SemaphoreType.DMA((8,)),
        ]
    return pl.pallas_call(
        kernel,
        out_shape=shapes,
        in_specs=[smem] * 3 + [anywhere] * 11,
        out_specs=[vmem] * len(shapes),
        scratch_shapes=scratch,
        cost_estimate=pl.CostEstimate(flops=1 << 30, bytes_accessed=6 << 20, transcendentals=1 << 20),
    )(at, where, live, near(held_a), *map(near, held_b), c, counts)


def name_of(notes, side, place, slot):
    return notes[side, place, slot].astype(jnp.int32)


def update_kernel(at_ref, *refs):
    all_refs, back_refs, outs, refs = refs[:9], refs[9:18], refs[18:21], refs[21:]
    grads, pieces, totals, notes, sems = refs
    members, slots, rows, _ = grads.shape[1:]
    side = members * rows
    copies = []
    for index in range(9):
        kind = 0 if index == 0 else 1
        to = pl.ds(0, members) if index == 0 else pl.ds(2 * (index - 1), 2)
        at = rows_at(at_ref[1 - kind], rows)
        copies.append(pltpu.make_async_copy(all_refs[index].at[:, side], notes.at[kind, to], sems.at[0, index]))
        copies.append(pltpu.make_async_copy(back_refs[index], grads.at[kind, to], sems.at[1, index]))
        copies.append(pltpu.make_async_copy(all_refs[index].at[:, at], pieces.at[kind, to], sems.at[2, index]))
    for copy in copies:
        copy.start()
    totals[...] = jnp.zeros_like(totals)
    for copy in copies:
        copy.wait()

    def gather(place, carry):
        for slot in range(slots):
            for kind in range(2):
                block = name_of(notes, kind, place, slot)
                totals[kind, block] = totals[kind, block] + grads[kind, place, slot]
        return carry

    lax.fori_loop(0, members, gather, 0)
    totals[0, :members] = pieces[0] - step_rate * totals[0, :members]
    for place in range(members):
        owner = at_ref[0] ^ place
        totals[1, owner] = pieces[1, place] - step_rate * totals[1, owner]

    def deal(index, carry):
        for way in range(2):
            place = 2 * index + way
            for slot in range(slots):
                outs[0][place, slot] = totals[0, jnp.minimum(name_of(notes, 0, place, slot), members - 1)]
                outs[1 + way][index, slot] = totals[1, jnp.minimum(name_of(notes, 1, place, slot), members - 1)]
            outs[0][place, slots] = totals[0, place]
            outs[1 + way][index, slots] = totals[1, at_ref[0] ^ place]
        return carry

    lax.fori_loop(0, members // 2, deal, 0)


def update(at, all_a, all_b, back_a, back_b):
    members, slots, rows, rank = back_a.shape
    half = shape_of(members // 2, slots + 1, rows, rank)
    return pl.pallas_call(
        update_kernel,
        out_shape=(shape_of(members, slots + 1, rows, rank), half, half),
        in_specs=[smem] + [anywhere] * 18,
        out_specs=(vmem, vmem, vmem),
        scratch_shapes=[
            pltpu.VMEM((2, members, slots, rows, rank), jnp.float32),
            pltpu.VMEM((2, members, rows, rank), jnp.float32),
            pltpu.VMEM((2, members + 1, rows, rank), jnp.float32),
            pltpu.SMEM((2, members, rank), jnp.float32),
            pltpu.SemaphoreType.DMA((3, 9)),
        ],
        cost_estimate=small_cost,
    )(at, *map(near, (all_a, *all_b, back_a, *back_b)))


def local(counts, block_coords, block_count, factor_a, factor_b, factor_c):
    assert STEPS == 2
    slots = counts.shape[2]
    members = lax.axis_size("row")
    side, rank = factor_a.shape
    at = jnp.stack([lax.axis_index("row"), lax.axis_index("col")]).astype(jnp.int32)
    where, live = block_coords, block_count
    counts = counts.reshape(counts.shape[2:])
    send_a, send_b = open_blocks(where, live, factor_a, factor_b, members)
    all_a = swap_col(send_a)
    both = jnp.stack([send_b, shift_row(send_b, 1)])
    all_b = [both] + [None] * len(chip_order)
    for pair in chip_order:
        all_b[pair] = shift_row(both, 2 * pair)
    grad_a, *grad_b = block_gradients(
        at, where, live, all_a, all_b, factor_c, counts, members, False
    )
    back_a = swap_col(grad_a)
    back_b = swap_row(*grad_b)
    dealt_a, *dealt_b = update(at, all_a, all_b, back_a, back_b)
    held_a = swap_col(dealt_a)
    held_b = swap_row(*dealt_b)
    grad_a, even_b, odd_b, base_b = block_gradients(at, where, live, held_a, held_b, factor_c, counts, members, True)
    terms_a = swap_col(grad_a)
    sums = even_b + shift_row(odd_b, 1)
    terms_b = [sums[0]]
    for pair in chip_order:
        terms_b.append(shift_row(sums[pair], 2 * pair))
    new_b = base_b - step_rate * sum(terms_b)
    new_a = held_a[:, slots].reshape(side, rank) - step_rate * terms_a.sum(0)
    return (new_a, new_b)


def solution(mesh):
    return jax.shard_map(
        local,
        mesh=mesh,
        in_specs=(
            P("row", "col", None, None, None, None),
            P(None, "row", "col", None),
            P("row", "col"),
            P(("row", "col"), None),
            P(("col", "row"), None),
            P(),
        ),
        out_specs=(P(("row", "col"), None), P(("col", "row"), None)),
        check_vma=False,
    )
```

```python
import functools

import jax
import jax.numpy as jnp
from jax import lax
from jax.experimental import pallas as pl
from jax.experimental.pallas import tpu as pltpu
from jax.sharding import PartitionSpec as P


STEPS = 2
step_rate = 0.004


vmem = pl.BlockSpec(memory_space=pltpu.VMEM)
smem = pl.BlockSpec(memory_space=pltpu.SMEM)
anywhere = pl.BlockSpec(memory_space=pl.ANY)
small_cost = pl.CostEstimate(flops=1 << 20, bytes_accessed=1 << 20, transcendentals=0)
parts = 2
chip_order = (6, 7, 5, 2, 4, 3, 1)


def shape_of(*sizes):
    return jax.ShapeDtypeStruct(sizes, jnp.float32)


def rows_at(index, rows):
    return pl.ds(pl.multiple_of(index * rows, rows), rows)


def split(value):
    high = value.astype(jnp.bfloat16)
    low = (value - high.astype(jnp.float32)).astype(jnp.bfloat16)
    return high, low


def two_halves(value):
    high, low = split(value)
    return jnp.concatenate([high, low], axis=1)


def pair_table(value):
    row = two_halves(value)
    return jnp.concatenate([row, row], axis=0)


def fold(product):
    return product[:, :128] + product[:, 128:]


def near(value):
    return pltpu.with_memory_space_constraint(value, pltpu.VMEM)


def swap_col(sent):
    return lax.all_to_all(sent, "col", 0, 0, tiled=True)


def shift_row(value, change):
    members = lax.axis_size("row")
    return lax.ppermute(value, "row", [(member, member ^ change) for member in range(members)])


def swap_row(even, odd):
    passed = shift_row(odd, 1)
    both = [jnp.stack([even[pair], passed[pair]]) for pair in range(even.shape[0])]
    got = [both[0]] + [None] * len(chip_order)
    for pair in chip_order:
        got[pair] = shift_row(both[pair], 2 * pair)
    return got


def open_kernel(where_ref, live_ref, a_ref, b_ref, send_a, send_b):
    slots = where_ref.shape[3]
    side, rank = a_ref.shape
    members = send_a.shape[0]
    rows = send_b.shape[0] - side
    lane = lax.broadcasted_iota(jnp.int32, (rows, rank), 1)

    def note(kind):
        value = jnp.zeros((rows, rank), jnp.float32)
        for slot in range(slots):
            named = jnp.where(slot < live_ref[0, 0], where_ref[kind, 0, 0, slot], members).astype(jnp.float32)
            value = jnp.where(lane == slot, named, value)
        return value

    send_b[:side] = b_ref[...]
    send_b[side:] = note(1)
    block, named = a_ref[...], note(0)
    for member in range(members):
        send_a[member, :side] = block
        send_a[member, side:] = named


def open_blocks(where, live, factor_a, factor_b, members):
    side, rank = factor_a.shape
    rows = side // members
    return pl.pallas_call(
        open_kernel,
        out_shape=(shape_of(members, side + rows, rank), shape_of(side + rows, rank)),
        in_specs=[smem, smem, vmem, vmem],
        out_specs=(vmem, vmem),
        cost_estimate=small_cost,
    )(where, live, factor_a, factor_b)


def slot_gradients(piece_a, piece_b, piece_c, observed):
    depth, (side, rank) = piece_c.shape[0], piece_a.shape
    b_high, b_low = split(piece_b)
    b_rows = jnp.concatenate(
        [jnp.concatenate([b_high, b_high], axis=1), jnp.concatenate([b_low, b_low], axis=1)], axis=0
    )
    b_table, a_table = pair_table(piece_b), pair_table(piece_a)
    counted = observed()
    grad_a = grad_b = jnp.zeros((side, rank), jnp.float32)
    each = depth // parts
    for part in range(parts):
        own = slice(part * each, (part + 1) * each)
        part_c = piece_c[own][:, None, :]
        scaled_a = (part_c * piece_a[None, :, :]).reshape(each * side, rank)
        model = fold(
            lax.dot_general(
                two_halves(scaled_a), b_rows, (((1,), (1,)), ((), ())), preferred_element_type=jnp.float32
            )
        )
        residual = jnp.exp(model) - counted[own].reshape(each * side, side).astype(jnp.float32)
        along_b = fold(jnp.dot(two_halves(residual), b_table, preferred_element_type=jnp.float32))
        turned = jnp.swapaxes(residual.reshape(each, side, side), 1, 2).reshape(each * side, side)
        along_a = fold(jnp.dot(two_halves(turned), a_table, preferred_element_type=jnp.float32))
        grad_a += (along_b.reshape(each, side, rank) * part_c).sum(0)
        grad_b += (along_a.reshape(each, side, rank) * part_c).sum(0)
    return grad_a, grad_b


class Fetches:
    def __init__(self, where_ref, live_ref, c_ref, counts_ref, part_c, seen, sems):
        self.refs = where_ref, live_ref, c_ref, counts_ref, part_c, seen, sems
        self.slots, self.depth = counts_ref.shape[:2]

    def copy_c(self, slot):
        where_ref, _, c_ref, _, part_c, _, sems = self.refs
        start_c = pl.multiple_of(where_ref[2, 0, 0, slot] * self.depth, self.depth)
        return pltpu.make_async_copy(c_ref.at[pl.ds(start_c, self.depth)], part_c.at[slot], sems.at[0, slot])

    def copy_counts(self, slot):
        _, _, _, counts_ref, _, seen, sems = self.refs
        return pltpu.make_async_copy(counts_ref.at[slot], seen.at[slot], sems.at[1, slot])

    def start(self):
        for slot in range(self.slots):

            @pl.when(slot < self.refs[1][0, 0])
            def _():
                self.copy_c(slot).start()
                self.copy_counts(slot).start()

    def factor(self, slot):
        self.copy_c(slot).wait()
        return self.refs[4][slot]

    def observed(self, slot):
        self.copy_counts(slot).wait()
        return self.refs[5][slot]


def first_kernel(at_ref, where_ref, live_ref, *refs):
    a_ref, b_refs, (c_ref, counts_ref), refs = refs[0], refs[1:9], refs[9:11], refs[11:]
    ga_ref, gb_refs, refs = refs[0], refs[1:3], refs[3:]
    all_b, turned_b, part_c, seen, sems = refs
    slots, _, side, rank = counts_ref.shape
    members = a_ref.shape[0]
    rows = side // members
    live = live_ref[0, 0]
    fetches = Fetches(where_ref, live_ref, c_ref, counts_ref, part_c, seen, sems)

    fetches.start()
    for place in range(members):
        all_b[place] = b_refs[place // 2][place % 2, :side]

    def visit(slot, carry):
        grad_a, grad_b = slot_gradients(
            a_ref[where_ref[0, 0, 0, slot], :side],
            all_b[where_ref[1, 0, 0, slot] ^ at_ref[0]],
            fetches.factor(slot),
            functools.partial(fetches.observed, slot),
        )
        ga_ref[:, slot] = grad_a.reshape(members, rows, rank)
        turned_b[...] = grad_b
        for place in range(members):
            gb_refs[place % 2][place // 2, slot] = turned_b[rows_at(at_ref[0] ^ place, rows), :]
        return carry

    lax.fori_loop(0, live, visit, 0)

    def clear(slot, carry):
        ga_ref[:, slot] = jnp.zeros((members, rows, rank), jnp.float32)
        for ref in gb_refs:
            ref[:, slot] = jnp.zeros((members // 2, rows, rank), jnp.float32)
        return carry

    lax.fori_loop(live, slots, clear, 0)


def last_kernel(at_ref, where_ref, live_ref, *refs):
    a_ref, b_refs, (c_ref, counts_ref), refs = refs[0], refs[1:9], refs[9:11], refs[11:]
    ga_ref, even_ref, odd_ref, base_b, refs = *refs[:4], refs[4:]
    block_b, part_c, seen, sems = refs
    slots, _, side, rank = counts_ref.shape
    members = a_ref.shape[0]
    rows = side // members
    live = live_ref[0, 0]
    me = at_ref[0]
    fetches = Fetches(where_ref, live_ref, c_ref, counts_ref, part_c, seen, sems)
    fetches.start()
    for ref in (ga_ref, even_ref, odd_ref):
        ref[...] = jnp.zeros_like(ref)
    for place in range(members):
        base_b[rows_at(me ^ place, rows), :] = b_refs[place // 2][place % 2, slots]

    def visit(slot, carry):
        for place in range(members):
            block_b[rows_at(me ^ place, rows), :] = b_refs[place // 2][place % 2, slot]
        grad_a, grad_b = slot_gradients(
            a_ref[:, slot].reshape(side, rank),
            block_b[...],
            fetches.factor(slot),
            functools.partial(fetches.observed, slot),
        )
        ga_ref[where_ref[0, 0, 0, slot]] += grad_a
        place = where_ref[1, 0, 0, slot] ^ me

        @pl.when(place % 2 == 0)
        def _():
            even_ref[place // 2] += grad_b

        @pl.when(place % 2 == 1)
        def _():
            odd_ref[place // 2] += grad_b

        return carry

    lax.fori_loop(0, live, visit, 0)


def block_gradients(at, where, live, held_a, held_b, c, counts, members, last):
    slots, depth, side, rank = counts.shape
    rows = side // members
    common = [
        pltpu.VMEM((slots, depth, rank), jnp.float32),
        pltpu.VMEM(counts.shape, jnp.int32),
        pltpu.SemaphoreType.DMA((2, slots)),
    ]
    if last:
        kernel = last_kernel
        half = shape_of(members // 2, side, rank)
        shapes = (shape_of(members, side, rank), half, half, shape_of(side, rank))
        scratch = [
            pltpu.VMEM((side, rank), jnp.float32),
            *common,
        ]
    else:
        kernel = first_kernel
        half = shape_of(members // 2, slots, rows, rank)
        shapes = (shape_of(members, slots, rows, rank), half, half)
        scratch = [
            pltpu.VMEM((members, side, rank), jnp.float32),
            pltpu.VMEM((side, rank), jnp.float32),
            *common,
        ]
    return pl.pallas_call(
        kernel,
        out_shape=shapes,
        in_specs=[smem] * 3 + [vmem] * 9 + [anywhere] * 2,
        out_specs=[vmem] * len(shapes),
        scratch_shapes=scratch,
        cost_estimate=pl.CostEstimate(flops=1 << 30, bytes_accessed=6 << 20, transcendentals=1 << 20),
    )(at, where, live, near(held_a), *map(near, held_b), c, counts)


def name_of(notes, side, place, slot):
    return notes[side, place, slot].astype(jnp.int32)


def update_kernel(at_ref, *refs):
    all_refs, back_refs, outs, refs = refs[:9], refs[9:18], refs[18:21], refs[21:]
    pieces, sums_a, sums_b, others_a, others_b, notes, sems = refs
    members, slots, rows, _ = back_refs[0].shape
    totals, others = (sums_a, sums_b), (others_a, others_b)
    side = members * rows
    copies = []
    for index in range(9):
        kind = 0 if index == 0 else 1
        to = pl.ds(0, members) if index == 0 else pl.ds(2 * (index - 1), 2)
        at = rows_at(at_ref[1 - kind], rows)
        copies.append(pltpu.make_async_copy(all_refs[index].at[:, side], notes.at[kind, to], sems.at[0, index]))
        copies.append(pltpu.make_async_copy(all_refs[index].at[:, at], pieces.at[kind, to], sems.at[1, index]))
    for copy in copies:
        copy.start()
    for ref in (*totals, *others):
        ref[...] = jnp.zeros_like(ref)
    for copy in copies:
        copy.wait()
    for place in range(members):
        sums = others if place % 2 else totals
        for slot in range(slots):
            for kind, grad in enumerate((back_refs[0][place, slot], back_refs[1 + place // 2][place % 2, slot])):
                block = name_of(notes, kind, place, slot)
                sums[kind][block] = sums[kind][block] + grad
    sums_a[:members] = pieces[0] - step_rate * (sums_a[:members] + others_a[:members])
    for place in range(members):
        owner = at_ref[0] ^ place
        sums_b[owner] = pieces[1, place] - step_rate * (sums_b[owner] + others_b[owner])

    def deal(index, carry):
        for way in range(2):
            place = 2 * index + way
            for slot in range(slots):
                outs[0][place, slot] = sums_a[jnp.minimum(name_of(notes, 0, place, slot), members - 1)]
                outs[1 + way][index, slot] = sums_b[jnp.minimum(name_of(notes, 1, place, slot), members - 1)]
            outs[0][place, slots] = sums_a[place]
            outs[1 + way][index, slots] = sums_b[at_ref[0] ^ place]
        return carry

    lax.fori_loop(0, members // 2, deal, 0)


def update(at, all_a, all_b, back_a, back_b):
    members, slots, rows, rank = back_a.shape
    half = shape_of(members // 2, slots + 1, rows, rank)
    return pl.pallas_call(
        update_kernel,
        out_shape=(shape_of(members, slots + 1, rows, rank), half, half),
        in_specs=[smem] + [anywhere] * 9 + [vmem] * 9,
        out_specs=(vmem, vmem, vmem),
        scratch_shapes=[
            pltpu.VMEM((2, members, rows, rank), jnp.float32),
            *[pltpu.VMEM((members + 1, rows, rank), jnp.float32)] * 4,
            pltpu.SMEM((2, members, rank), jnp.float32),
            pltpu.SemaphoreType.DMA((2, 9)),
        ],
        cost_estimate=small_cost,
    )(at, *map(near, (all_a, *all_b, back_a, *back_b)))


def local(counts, block_coords, block_count, factor_a, factor_b, factor_c):
    assert STEPS == 2
    slots = counts.shape[2]
    members = lax.axis_size("row")
    side, rank = factor_a.shape
    at = jnp.stack([lax.axis_index("row"), lax.axis_index("col")]).astype(jnp.int32)
    where, live = block_coords, block_count
    counts = counts.reshape(counts.shape[2:])
    send_a, send_b = open_blocks(where, live, factor_a, factor_b, members)
    all_a = swap_col(send_a)
    both = jnp.stack([send_b, shift_row(send_b, 1)])
    all_b = [both] + [None] * len(chip_order)
    for pair in chip_order:
        all_b[pair] = shift_row(both, 2 * pair)
    grad_a, *grad_b = block_gradients(
        at, where, live, all_a, all_b, factor_c, counts, members, False
    )
    back_a = swap_col(grad_a)
    back_b = swap_row(*grad_b)
    dealt_a, *dealt_b = update(at, all_a, all_b, back_a, back_b)
    held_a = swap_col(dealt_a)
    held_b = swap_row(*dealt_b)
    grad_a, even_b, odd_b, base_b = block_gradients(at, where, live, held_a, held_b, factor_c, counts, members, True)
    terms_a = swap_col(grad_a)
    sums = even_b + shift_row(odd_b, 1)
    terms_b = [sums[0]]
    for pair in chip_order:
        terms_b.append(shift_row(sums[pair], 2 * pair))
    new_b = base_b - step_rate * sum(terms_b)
    new_a = held_a[:, slots].reshape(side, rank) - step_rate * terms_a.sum(0)
    return (new_a, new_b)


def solution(mesh):
    return jax.shard_map(
        local,
        mesh=mesh,
        in_specs=(
            P("row", "col", None, None, None, None),
            P(None, "row", "col", None),
            P("row", "col"),
            P(("row", "col"), None),
            P(("col", "row"), None),
            P(),
        ),
        out_specs=(P(("row", "col"), None), P(("col", "row"), None)),
        check_vma=False,
    )
```

```python
import functools

import jax
import jax.numpy as jnp
from jax import lax
from jax.experimental import pallas as pl
from jax.experimental.pallas import tpu as pltpu
from jax.sharding import PartitionSpec as P


STEPS = 2
step_rate = 0.004


vmem = pl.BlockSpec(memory_space=pltpu.VMEM)
smem = pl.BlockSpec(memory_space=pltpu.SMEM)
anywhere = pl.BlockSpec(memory_space=pl.ANY)
small_cost = pl.CostEstimate(flops=1 << 20, bytes_accessed=1 << 20, transcendentals=0)
parts = 2
chip_order = (6, 7, 5, 2, 4, 3, 1)


def shape_of(*sizes):
    return jax.ShapeDtypeStruct(sizes, jnp.float32)


def rows_at(index, rows):
    return pl.ds(pl.multiple_of(index * rows, rows), rows)


def split(value):
    high = value.astype(jnp.bfloat16)
    low = (value - high.astype(jnp.float32)).astype(jnp.bfloat16)
    return high, low


def two_halves(value):
    high, low = split(value)
    return jnp.concatenate([high, low], axis=1)


def pair_table(value):
    row = two_halves(value)
    return jnp.concatenate([row, row], axis=0)


def fold(product):
    return product[:, :128] + product[:, 128:]


def near(value):
    return pltpu.with_memory_space_constraint(value, pltpu.VMEM)


def swap_col(sent):
    return lax.all_to_all(sent, "col", 0, 0, tiled=True)


def shift_row(value, change):
    members = lax.axis_size("row")
    return lax.ppermute(value, "row", [(member, member ^ change) for member in range(members)])


def swap_row(even, odd):
    passed = shift_row(odd, 1)
    both = [jnp.stack([even[pair], passed[pair]]) for pair in range(even.shape[0])]
    got = [both[0]] + [None] * len(chip_order)
    for pair in chip_order:
        got[pair] = shift_row(both[pair], 2 * pair)
    return got


def open_kernel(where_ref, live_ref, a_ref, b_ref, send_a, send_b):
    slots = where_ref.shape[3]
    side, rank = a_ref.shape
    members = send_a.shape[0]
    rows = send_b.shape[0] - side
    lane = lax.broadcasted_iota(jnp.int32, (rows, rank), 1)

    def note(kind):
        value = jnp.zeros((rows, rank), jnp.float32)
        for slot in range(slots):
            named = jnp.where(slot < live_ref[0, 0], where_ref[kind, 0, 0, slot], members).astype(jnp.float32)
            value = jnp.where(lane == slot, named, value)
        return value

    send_b[:side] = b_ref[...]
    send_b[side:] = note(1)
    block, named = a_ref[...], note(0)
    for member in range(members):
        send_a[member, :side] = block
        send_a[member, side:] = named


def open_blocks(where, live, factor_a, factor_b, members):
    side, rank = factor_a.shape
    rows = side // members
    return pl.pallas_call(
        open_kernel,
        out_shape=(shape_of(members, side + rows, rank), shape_of(side + rows, rank)),
        in_specs=[smem, smem, vmem, vmem],
        out_specs=(vmem, vmem),
        cost_estimate=small_cost,
    )(where, live, factor_a, factor_b)


def slot_gradients(piece_a, piece_b, piece_c, observed):
    depth, (side, rank) = piece_c.shape[0], piece_a.shape
    b_high, b_low = split(piece_b)
    b_rows = jnp.concatenate(
        [jnp.concatenate([b_high, b_high], axis=1), jnp.concatenate([b_low, b_low], axis=1)], axis=0
    )
    b_table, a_table = pair_table(piece_b), pair_table(piece_a)
    counted = observed()
    grad_a = grad_b = jnp.zeros((side, rank), jnp.float32)
    each = depth // parts
    for part in range(parts):
        own = slice(part * each, (part + 1) * each)
        part_c = piece_c[own][:, None, :]
        scaled_a = (part_c * piece_a[None, :, :]).reshape(each * side, rank)
        model = fold(
            lax.dot_general(
                two_halves(scaled_a), b_rows, (((1,), (1,)), ((), ())), preferred_element_type=jnp.float32
            )
        )
        residual = jnp.exp(model) - counted[own].reshape(each * side, side).astype(jnp.float32)
        along_b = fold(jnp.dot(two_halves(residual), b_table, preferred_element_type=jnp.float32))
        turned = jnp.swapaxes(residual.reshape(each, side, side), 1, 2).reshape(each * side, side)
        along_a = fold(jnp.dot(two_halves(turned), a_table, preferred_element_type=jnp.float32))
        grad_a += (along_b.reshape(each, side, rank) * part_c).sum(0)
        grad_b += (along_a.reshape(each, side, rank) * part_c).sum(0)
    return grad_a, grad_b


class Fetches:
    def __init__(self, where_ref, live_ref, c_ref, counts_ref, part_c, seen, sems):
        self.refs = where_ref, live_ref, c_ref, counts_ref, part_c, seen, sems
        self.slots, self.depth = counts_ref.shape[:2]

    def copy_c(self, slot):
        where_ref, _, c_ref, _, part_c, _, sems = self.refs
        start_c = pl.multiple_of(where_ref[2, 0, 0, slot] * self.depth, self.depth)
        return pltpu.make_async_copy(c_ref.at[pl.ds(start_c, self.depth)], part_c.at[slot], sems.at[0, slot])

    def copy_counts(self, slot):
        _, _, _, counts_ref, _, seen, sems = self.refs
        return pltpu.make_async_copy(counts_ref.at[slot], seen.at[slot], sems.at[1, slot])

    def start(self):
        for slot in range(self.slots):

            @pl.when(slot < self.refs[1][0, 0])
            def _():
                self.copy_c(slot).start()
                self.copy_counts(slot).start()

    def factor(self, slot):
        self.copy_c(slot).wait()
        return self.refs[4][slot]

    def observed(self, slot):
        self.copy_counts(slot).wait()
        return self.refs[5][slot]


def first_kernel(at_ref, where_ref, live_ref, *refs):
    a_ref, b_refs, (c_ref, counts_ref), refs = refs[0], refs[1:9], refs[9:11], refs[11:]
    ga_ref, gb_refs, refs = refs[0], refs[1:3], refs[3:]
    all_b, turned_b, part_c, seen, sems = refs
    slots, _, side, rank = counts_ref.shape
    members = a_ref.shape[0]
    rows = side // members
    live = live_ref[0, 0]
    fetches = Fetches(where_ref, live_ref, c_ref, counts_ref, part_c, seen, sems)

    fetches.start()
    for place in range(members):
        all_b[place] = b_refs[place // 2][place % 2, :side]

    def visit(slot, carry):
        grad_a, grad_b = slot_gradients(
            a_ref[where_ref[0, 0, 0, slot], :side],
            all_b[where_ref[1, 0, 0, slot] ^ at_ref[0]],
            fetches.factor(slot),
            functools.partial(fetches.observed, slot),
        )
        ga_ref[:, slot] = grad_a.reshape(members, rows, rank)
        turned_b[...] = grad_b
        for place in range(members):
            gb_refs[place % 2][place // 2, slot] = turned_b[rows_at(at_ref[0] ^ place, rows), :]
        return carry

    lax.fori_loop(0, live, visit, 0)

    def clear(slot, carry):
        ga_ref[:, slot] = jnp.zeros((members, rows, rank), jnp.float32)
        for ref in gb_refs:
            ref[:, slot] = jnp.zeros((members // 2, rows, rank), jnp.float32)
        return carry

    lax.fori_loop(live, slots, clear, 0)


def last_kernel(at_ref, where_ref, live_ref, *refs):
    a_ref, b_refs, (c_ref, counts_ref), refs = refs[0], refs[1:9], refs[9:11], refs[11:]
    ga_ref, even_ref, odd_ref, base_b, refs = *refs[:4], refs[4:]
    block_b, part_c, seen, sems = refs
    slots, _, side, rank = counts_ref.shape
    members = a_ref.shape[0]
    rows = side // members
    live = live_ref[0, 0]
    me = at_ref[0]
    fetches = Fetches(where_ref, live_ref, c_ref, counts_ref, part_c, seen, sems)
    fetches.start()
    for ref in (ga_ref, even_ref, odd_ref):
        ref[...] = jnp.zeros_like(ref)
    for place in range(members):
        base_b[rows_at(me ^ place, rows), :] = b_refs[place // 2][place % 2, slots]

    def visit(slot, carry):
        for place in range(members):
            block_b[rows_at(me ^ place, rows), :] = b_refs[place // 2][place % 2, slot]
        grad_a, grad_b = slot_gradients(
            a_ref[:, slot].reshape(side, rank),
            block_b[...],
            fetches.factor(slot),
            functools.partial(fetches.observed, slot),
        )
        ga_ref[where_ref[0, 0, 0, slot]] += grad_a
        place = where_ref[1, 0, 0, slot] ^ me

        @pl.when(place % 2 == 0)
        def _():
            even_ref[place // 2] += grad_b

        @pl.when(place % 2 == 1)
        def _():
            odd_ref[place // 2] += grad_b

        return carry

    lax.fori_loop(0, live, visit, 0)


def block_gradients(at, where, live, held_a, held_b, c, counts, members, last):
    slots, depth, side, rank = counts.shape
    rows = side // members
    common = [
        pltpu.VMEM((slots, depth, rank), jnp.float32),
        pltpu.VMEM(counts.shape, jnp.int32),
        pltpu.SemaphoreType.DMA((2, slots)),
    ]
    if last:
        kernel = last_kernel
        half = shape_of(members // 2, side, rank)
        shapes = (shape_of(members, side, rank), half, half, shape_of(side, rank))
        scratch = [
            pltpu.VMEM((side, rank), jnp.float32),
            *common,
        ]
    else:
        kernel = first_kernel
        half = shape_of(members // 2, slots, rows, rank)
        shapes = (shape_of(members, slots, rows, rank), half, half)
        scratch = [
            pltpu.VMEM((members, side, rank), jnp.float32),
            pltpu.VMEM((side, rank), jnp.float32),
            *common,
        ]
    return pl.pallas_call(
        kernel,
        out_shape=shapes,
        in_specs=[smem] * 3 + [vmem] * 9 + [anywhere] * 2,
        out_specs=[vmem] * len(shapes),
        scratch_shapes=scratch,
        cost_estimate=pl.CostEstimate(flops=1 << 30, bytes_accessed=6 << 20, transcendentals=1 << 20),
    )(at, where, live, near(held_a), *map(near, held_b), c, counts)


def name_of(notes, side, place, slot):
    return notes[side, place, slot].astype(jnp.int32)


def update_kernel(at_ref, *refs):
    all_refs, back_refs, outs, refs = refs[:9], refs[9:18], refs[18:21], refs[21:]
    pieces, sums_a, sums_b, others_a, others_b, notes, names, sems = refs
    members, slots, rows, _ = back_refs[0].shape
    totals, others = (sums_a, sums_b), (others_a, others_b)
    side = members * rows
    copies = []
    for index in range(9):
        kind = 0 if index == 0 else 1
        to = pl.ds(0, members) if index == 0 else pl.ds(2 * (index - 1), 2)
        at = rows_at(at_ref[1 - kind], rows)
        copies.append(pltpu.make_async_copy(all_refs[index].at[:, side], notes.at[kind, to], sems.at[0, index]))
        copies.append(pltpu.make_async_copy(all_refs[index].at[:, at], pieces.at[kind, to], sems.at[1, index]))
    for copy in copies:
        copy.start()
    for ref in (*totals, *others):
        ref[...] = jnp.zeros_like(ref)
    for copy in copies:
        copy.wait()
    for place in range(members):
        sums = others if place % 2 else totals
        for slot in range(slots):
            for kind, grad in enumerate((back_refs[0][place, slot], back_refs[1 + place // 2][place % 2, slot])):
                block = name_of(notes, kind, place, slot)
                names[kind, place, slot] = jnp.minimum(block, members - 1)
                sums[kind][block] = sums[kind][block] + grad
    sums_a[:members] = pieces[0] - step_rate * (sums_a[:members] + others_a[:members])
    for place in range(members):
        owner = at_ref[0] ^ place
        sums_b[owner] = pieces[1, place] - step_rate * (sums_b[owner] + others_b[owner])

    for place in range(members):
        out_b = outs[1 + place % 2].at[place // 2]
        for slot in range(slots):
            outs[0][place, slot] = sums_a[names[0, place, slot]]
            out_b[slot] = sums_b[names[1, place, slot]]
        outs[0][place, slots] = sums_a[place]
        out_b[slots] = sums_b[at_ref[0] ^ place]


def update(at, all_a, all_b, back_a, back_b):
    members, slots, rows, rank = back_a.shape
    half = shape_of(members // 2, slots + 1, rows, rank)
    return pl.pallas_call(
        update_kernel,
        out_shape=(shape_of(members, slots + 1, rows, rank), half, half),
        in_specs=[smem] + [anywhere] * 9 + [vmem] * 9,
        out_specs=(vmem, vmem, vmem),
        scratch_shapes=[
            pltpu.VMEM((2, members, rows, rank), jnp.float32),
            *[pltpu.VMEM((members + 1, rows, rank), jnp.float32)] * 4,
            pltpu.SMEM((2, members, rank), jnp.float32),
            pltpu.SMEM((2, members, slots), jnp.int32),
            pltpu.SemaphoreType.DMA((2, 9)),
        ],
        cost_estimate=small_cost,
    )(at, *map(near, (all_a, *all_b, back_a, *back_b)))


def local(counts, block_coords, block_count, factor_a, factor_b, factor_c):
    assert STEPS == 2
    slots = counts.shape[2]
    members = lax.axis_size("row")
    side, rank = factor_a.shape
    at = jnp.stack([lax.axis_index("row"), lax.axis_index("col")]).astype(jnp.int32)
    where, live = block_coords, block_count
    counts = counts.reshape(counts.shape[2:])
    send_a, send_b = open_blocks(where, live, factor_a, factor_b, members)
    all_a = swap_col(send_a)
    both = jnp.stack([send_b, shift_row(send_b, 1)])
    all_b = [both] + [None] * len(chip_order)
    for pair in chip_order:
        all_b[pair] = shift_row(both, 2 * pair)
    grad_a, *grad_b = block_gradients(
        at, where, live, all_a, all_b, factor_c, counts, members, False
    )
    back_a = swap_col(grad_a)
    back_b = swap_row(*grad_b)
    dealt_a, *dealt_b = update(at, all_a, all_b, back_a, back_b)
    held_a = swap_col(dealt_a)
    held_b = swap_row(*dealt_b)
    grad_a, even_b, odd_b, base_b = block_gradients(
        at, where, live, held_a, held_b, factor_c, counts, members, True
    )
    terms_a = swap_col(grad_a)
    sums = even_b + shift_row(odd_b, 1)
    terms_b = [sums[0]]
    for pair in chip_order:
        terms_b.append(shift_row(sums[pair], 2 * pair))
    new_b = base_b - step_rate * sum(terms_b)
    new_a = held_a[:, slots].reshape(side, rank) - step_rate * terms_a.sum(0)
    return (new_a, new_b)


def solution(mesh):
    return jax.shard_map(
        local,
        mesh=mesh,
        in_specs=(
            P("row", "col", None, None, None, None),
            P(None, "row", "col", None),
            P("row", "col"),
            P(("row", "col"), None),
            P(("col", "row"), None),
            P(),
        ),
        out_specs=(P(("row", "col"), None), P(("col", "row"), None)),
        check_vma=False,
    )
```
